32 devices in a mesh: slab: 8 (over y, x, core), space: 4 (over z).
Axes of the slice: x: 2, y: 2, z: 4, core: 2. Of those that a mesh axis runs over, the one named last changes fastest.
Arguments:
- query_rows: bfloat16 [8192, 128], P(('slab', 'space')), may hold values from -4 to 4, as said below
- key_rows: bfloat16 [8192, 128], P(('slab', 'space')), may hold values from -4 to 4, as said below
- value_rows: bfloat16 [8192, 128], P(('slab', 'space')), may hold values from -6 to 6
- out_saved: bfloat16 [8192, 128], P(('slab', 'space')), may hold values from -1.796875 to 1.796875
- grad_out: bfloat16 [8192, 128], P(('slab', 'space')), may hold values from -6 to 6
- log_norm: float32 [1, 8192], P(None, ('slab', 'space')), as said below
- band_mask: int32 [6, 8, 8], replicated, may hold values from 0 to 1, as said below
- frame_of_slab: int32 [8], replicated, may hold values from 0 to 7, as said below
Outputs:
- grad_query: bfloat16 [8192, 128], P(('slab', 'space'))
- grad_key: bfloat16 [8192, 128], P(('slab', 'space'))
- grad_value: bfloat16 [8192, 128], P(('slab', 'space'))
The draws below stay inside these ranges and needn't reach their ends.
Inputs may be any that keep to these rules, and one draw needn't show every extreme that they name: query_rows are drawn afresh for each token. key_rows are drawn afresh for each token. log_norm[h, t] is the log of the sum over u with allowed[t, u] = 1 of exp(q_h(t) . k_h(u) / sqrt(128)) for the given queries and keys. band_mask[0, a, b] = 1 whenever tiles a and b differ by at most 1; band_mask[0, a, b] is 0 unless a // 2 and b // 2 differ by at most 1; for levels 1 and up, band_mask[l, a, b] is 0 unless a // 2 and b // 2 are equal. frame_of_slab names every frame once.
All inputs are finite; a program needn't handle non-finite values.
Results may differ from the reference program's by a relative error of at most 0.0075.
Values may be sent and summed in bfloat16 or wider, within the bound.
No kernel may reach another device: no remote copies, remote signals or barrier semaphores. Data moves between devices by JAX's collectives and lax.ppermute only.
A program may use at most 64 MiB of HBM per device.

```python
import jax
import jax.numpy as jnp
from jax import lax

HEAD_DIM = 128
HEADS = 1
TILE = 128
LEVELS = 6
TOK_DEV = 256
TILES = 8
TOKENS = 8192
N_SLAB = 8
N_SPACE = 4


def frame_order(key):
    return jax.random.permutation(jax.random.fold_in(key, 11), N_SLAB).astype(jnp.int32)


def tile_pattern(key):
    per_device = TOK_DEV // TILE
    levels = jnp.arange(LEVELS, dtype=jnp.int32)
    tiles = jnp.arange(TILES, dtype=jnp.int32) // per_device
    apart = jnp.abs(tiles[:, None] - tiles[None, :])
    limits = jnp.where(levels == 0, jnp.int32(1 << 15), jnp.right_shift(jnp.int32(1 << 16), jnp.maximum(levels - 1, 0)))
    picks = jax.random.randint(jax.random.fold_in(key, 13), (LEVELS, TILES, TILES), 0, 1 << 16, dtype=jnp.int32)
    reach = jnp.where(levels[:, None, None] == 0, apart[None] <= 1, apart[None] == 0)
    chosen = reach & (picks < limits[:, None, None])
    tile_ids = jnp.arange(TILES, dtype=jnp.int32)
    near_tile = jnp.abs(tile_ids[:, None] - tile_ids[None, :]) <= 1
    diagonal = (levels[:, None, None] == 0) & near_tile[None]
    return (chosen | diagonal).astype(jnp.int32)


def token_rows(key, salt):
    shape = (TOKENS, HEADS * HEAD_DIM)
    rows = jax.random.truncated_normal(jax.random.fold_in(key, salt), -4.0, 4.0, shape, jnp.float32)
    return rows.astype(jnp.bfloat16)


def draw_query_rows(key, part):
    return token_rows(key, 21)


def draw_key_rows(key, part):
    return token_rows(key, 31)


def draw_band_mask(key, part):
    return tile_pattern(key)


def draw_frame_of_slab(key, part):
    return frame_order(key)


def draw_log_norm(key, part):
    per_device = TOK_DEV // TILE
    score_scale = HEAD_DIM ** (-0.5)
    queries = token_rows(key, 21).astype(jnp.float32).reshape(N_SLAB, N_SPACE, TOK_DEV, HEADS, HEAD_DIM)
    keys_all = token_rows(key, 31).astype(jnp.float32).reshape(N_SLAB, N_SPACE, TOK_DEV, HEADS, HEAD_DIM)
    pattern = tile_pattern(key)
    frames = frame_order(key)
    padded_mask = jnp.pad(pattern[0], ((0, 0), (per_device, per_device)))

    def window_of(column):
        start = column * per_device
        return lax.dynamic_slice(padded_mask, (start, start), (per_device, 3 * per_device))
    window_tiles = jax.vmap(window_of)(jnp.arange(N_SPACE, dtype=jnp.int32))
    window_allow = jnp.repeat(jnp.repeat(window_tiles, TILE, axis=-2), TILE, axis=-1) > 0
    padded_keys = jnp.pad(keys_all, ((0, 0), (1, 1), (0, 0), (0, 0), (0, 0)))
    wide_keys = jnp.concatenate([padded_keys[:, :-2], padded_keys[:, 1:-1], padded_keys[:, 2:]], axis=2)
    scores = jnp.einsum('spqhd,spkhd->sphqk', queries, wide_keys) * score_scale
    total = jax.nn.logsumexp(jnp.where(window_allow[None, :, None], scores, -jnp.inf), axis=-1)
    level_tiles = jnp.moveaxis(jnp.diagonal(pattern.reshape(LEVELS, N_SPACE, per_device, N_SPACE, per_device), axis1=1, axis2=3), -1, 1)
    level_allow = jnp.repeat(jnp.repeat(level_tiles, TILE, axis=-2), TILE, axis=-1) > 0
    slab_ids = jnp.arange(N_SLAB, dtype=jnp.int32)
    powers = jnp.left_shift(jnp.int32(1), jnp.arange(LEVELS - 1, dtype=jnp.int32))

    def cycle_offset(running, offset):
        source = (slab_ids - offset) % N_SLAB
        distance = jnp.abs(frames - frames[source])
        level = jnp.sum((distance[:, None] >= powers[None]).astype(jnp.int32), axis=1)
        allow = level_allow[level]
        pair_scores = jnp.einsum('spqhd,spkhd->sphqk', queries, keys_all[source]) * score_scale
        piece = jax.nn.logsumexp(jnp.where(allow[:, :, None], pair_scores, -jnp.inf), axis=-1)
        return (jnp.logaddexp(running, piece), None)
    total, unused = lax.scan(cycle_offset, total, jnp.arange(1, N_SLAB, dtype=jnp.int32))
    return total.transpose(2, 0, 1, 3).reshape(HEADS, TOKENS).astype(jnp.float32)


def steps_of(stream_key, shape, cuts, least, high):
    def one(position, shards_of):
        draws = jax.random.uniform(jax.random.fold_in(jax.random.fold_in(stream_key, 6), position), (shards_of,), jnp.float32, least / len(cuts), high / len(cuts))
        return jnp.repeat(jnp.exp(draws), shape[position] // shards_of).reshape((-1,) + (1,) * (len(shape) - position - 1))

    loudness = one(*cuts[0])
    for cut in cuts[1:]:
        loudness = loudness * one(*cut)
    return loudness


def scatter_about(own_key, dims, scale, most, cuts=(), kind=jnp.bfloat16):
    drawn = scale * jax.random.normal(own_key, dims, jnp.float32)
    if cuts:
        drawn = drawn * steps_of(own_key, dims, cuts, -0.22, 0.18)
    return jnp.clip(drawn, -most, most).astype(kind)


def setup_inputs(seed: int = 0) -> dict:
    seeds = jax.random.split(jax.random.key(seed), 9)
    return {
        "query_rows": draw_query_rows(jax.random.fold_in(seeds[8], 71), 0),
        "key_rows": draw_key_rows(jax.random.fold_in(seeds[8], 71), 0),
        "value_rows": scatter_about(seeds[2], (TOKENS, HEADS * HEAD_DIM), 1.0, 6.0, ((0, 32),)),
        "out_saved": scatter_about(seeds[3], (TOKENS, HEADS * HEAD_DIM), 0.3, 1.796875, ((0, 32),)),
        "grad_out": scatter_about(seeds[4], (TOKENS, HEADS * HEAD_DIM), 1.0, 6.0, ((0, 32),)),
        "log_norm": draw_log_norm(jax.random.fold_in(seeds[8], 71), 0),
        "band_mask": draw_band_mask(jax.random.fold_in(seeds[8], 71), 0),
        "frame_of_slab": draw_frame_of_slab(jax.random.fold_in(seeds[8], 71), 0),
    }


def expand_tiles(tile_mask, tile):
    return jnp.repeat(jnp.repeat(tile_mask, tile, axis=-2), tile, axis=-1) > 0


def level_of(distance, level_count):
    powers = jnp.left_shift(jnp.int32(1), jnp.arange(level_count - 1, dtype=jnp.int32))
    return jnp.sum((distance[..., None] >= powers).astype(jnp.int32), axis=-1)


def rounded(values_wide):
    half = values_wide.astype(jnp.bfloat16)
    return lax.optimization_barrier(half).astype(jnp.float32)


def block_grads(query, grad_rows, log_norm, delta, key_block, value_block, allow):
    head_count = log_norm.shape[0]
    query_count = query.shape[0]
    key_count = key_block.shape[0]
    head_dim = query.shape[1] // head_count
    score_scale = head_dim ** -0.5
    query_f = query.astype(jnp.float32).reshape(query_count, head_count, head_dim)
    grad_f = grad_rows.astype(jnp.float32).reshape(query_count, head_count, head_dim)
    key_f = key_block.astype(jnp.float32).reshape(key_count, head_count, head_dim)
    value_f = value_block.astype(jnp.float32).reshape(key_count, head_count, head_dim)
    scores = jnp.einsum("qhd,khd->hqk", query_f, key_f) * score_scale
    prob = jnp.where(allow[None], jnp.exp(scores - log_norm[:, :, None]), 0.0)
    dprob = jnp.einsum("qhd,khd->hqk", grad_f, value_f)
    dscore = prob * (dprob - delta[:, :, None])
    prob_half = rounded(prob)
    score_half = rounded(dscore)
    grad_query = jnp.einsum("hqk,khd->qhd", score_half, key_f).reshape(query_count, -1) * score_scale
    grad_key = jnp.einsum("hqk,qhd->khd", score_half, query_f).reshape(key_count, -1) * score_scale
    grad_value = jnp.einsum("hqk,qhd->khd", prob_half, grad_f).reshape(key_count, -1)
    return grad_query, grad_key, grad_value


def reference(query_rows, key_rows, value_rows, out_saved, grad_out, log_norm, band_mask, frame_of_slab):
    per_device = TOK_DEV // TILE
    width = HEADS * HEAD_DIM

    def blocks(rows):
        return rows.reshape(N_SLAB, N_SPACE, TOK_DEV, width)

    query_b = blocks(query_rows)
    key_b = blocks(key_rows)
    value_b = blocks(value_rows)
    grad_b = blocks(grad_out)
    stats = log_norm.reshape(HEADS, N_SLAB, N_SPACE, TOK_DEV).transpose(1, 2, 0, 3)
    product = grad_out.astype(jnp.float32) * out_saved.astype(jnp.float32)
    delta = product.reshape(N_SLAB, N_SPACE, TOK_DEV, HEADS, HEAD_DIM).sum(-1).transpose(0, 1, 3, 2)

    padded_mask = jnp.pad(band_mask[0], ((0, 0), (per_device, per_device)))
    columns = jnp.arange(N_SPACE, dtype=jnp.int32)

    def window_of(column):
        start = (column * per_device).astype(jnp.int32)
        return lax.dynamic_slice(padded_mask, (start, start), (per_device, 3 * per_device))

    window_allow = expand_tiles(jax.vmap(window_of)(columns), TILE)

    def widen(rows):
        padded = jnp.pad(rows, ((0, 0), (1, 1), (0, 0), (0, 0)))
        return jnp.concatenate([padded[:, :-2], padded[:, 1:-1], padded[:, 2:]], axis=2)

    inner = jax.vmap(block_grads, in_axes=(0, 0, 0, 0, 0, 0, 0))

    def window_slab(args):
        return inner(args[0], args[1], args[2], args[3], args[4], args[5], window_allow)

    win_q, win_k, win_v = lax.map(window_slab, (query_b, grad_b, stats, delta, widen(key_b), widen(value_b)))

    def fold_back(wide):
        own = wide[:, :, TOK_DEV:2 * TOK_DEV]
        from_lower = jnp.pad(wide[:, :, 2 * TOK_DEV:], ((0, 0), (1, 0), (0, 0), (0, 0)))[:, :-1]
        from_upper = jnp.pad(wide[:, :, :TOK_DEV], ((0, 0), (0, 1), (0, 0), (0, 0)))[:, 1:]
        return own + from_lower + from_upper

    level_tiles = jnp.moveaxis(jnp.diagonal(band_mask.reshape(LEVELS, N_SPACE, per_device, N_SPACE, per_device), axis1=1, axis2=3), -1, 1)
    level_allow = expand_tiles(level_tiles, TILE)
    slab_ids = jnp.arange(N_SLAB, dtype=jnp.int32)
    pair_grads = jax.vmap(jax.vmap(block_grads))

    def cycle_offset(sums, offset):
        grad_q, grad_k, grad_v = sums
        source = (slab_ids - offset) % N_SLAB
        level = level_of(jnp.abs(frame_of_slab - frame_of_slab[source]), LEVELS)
        part_q, part_k, part_v = pair_grads(query_b, grad_b, stats, delta, key_b[source], value_b[source], level_allow[level])
        return (grad_q + part_q, grad_k.at[source].add(part_k), grad_v.at[source].add(part_v)), None

    start = (win_q, fold_back(win_k), fold_back(win_v))
    sums, unused = lax.scan(cycle_offset, start, jnp.arange(1, N_SLAB, dtype=jnp.int32))
    grad_q, grad_k, grad_v = sums
    return (grad_q.reshape(TOKENS, width).astype(jnp.bfloat16),
            grad_k.reshape(TOKENS, width).astype(jnp.bfloat16),
            grad_v.reshape(TOKENS, width).astype(jnp.bfloat16))
```

```python
import functools

import jax
import jax.numpy as jnp
from jax import lax
from jax.experimental import pallas as pl
from jax.experimental.pallas import tpu as pltpu
from jax.sharding import PartitionSpec as P

TILE = 128
LOG2E = 1.4426950408889634
FAR = 1e30
STAT_ROWS = 16
VMEM = pl.BlockSpec(memory_space=pltpu.VMEM)
SMEM = pl.BlockSpec(memory_space=pltpu.SMEM)
F32 = jnp.float32
BF16 = jnp.bfloat16


def thirds(row):
    high = row.astype(BF16)
    rest = row - high.astype(F32)
    middle = rest.astype(BF16)
    low = (rest - middle.astype(F32)).astype(BF16)
    return [high.astype(F32), middle.astype(F32), low.astype(F32)]


def pack_kernel(q_ref, k_ref, v_ref, o_ref, do_ref, lse_ref, query_ref, key_ref, all_ref):
    rows = q_ref.shape[0]
    width = q_ref.shape[1]
    product = do_ref[...].astype(F32) * o_ref[...].astype(F32)
    delta = jnp.sum(product.T, axis=0, keepdims=True)
    norm = lse_ref[...] * LOG2E
    parts = []
    for row in (norm, delta):
        for third in thirds(row):
            for start in range(0, rows, width):
                parts.append(third[:, start : start + width])
    parts.append(jnp.zeros((STAT_ROWS - len(parts), width), F32))
    stats = jnp.concatenate(parts, axis=0).astype(BF16)
    query = q_ref[...]
    grad = do_ref[...]
    keys = k_ref[...]
    values = v_ref[...]
    for ref in (query_ref, all_ref):
        ref[0:rows] = query
        ref[rows : 2 * rows] = grad
        ref[2 * rows : 2 * rows + STAT_ROWS] = stats
    base = 2 * rows + STAT_ROWS
    key_ref[0:rows] = keys
    key_ref[rows : 2 * rows] = values
    all_ref[base : base + rows] = keys
    all_ref[base + rows : base + 2 * rows] = values


class Queries:
    def __init__(self, ref, rows):
        width = ref.shape[1]
        self.query = ref[0:rows]
        self.grad = ref[rows : 2 * rows]
        stats = ref[2 * rows : 2 * rows + STAT_ROWS].astype(F32)
        pieces = rows // width

        def joined(first):
            lines = []
            for piece in range(pieces):
                at = [first + third * pieces + piece for third in range(3)]
                lines.append(sum(stats[i : i + 1] for i in at))
            return jnp.concatenate(lines, axis=1)

        self.norm = joined(0)
        self.delta = joined(3 * pieces)


class Keys:
    def __init__(self, ref, rows, base=0):
        self.key = ref[base : base + rows]
        self.value = ref[base + rows : base + 2 * rows]


def dot_nt(a, b):
    return lax.dot_general(a, b, (((1,), (1,)), ((), ())), preferred_element_type=F32)


def dot_nn(a, b):
    return lax.dot_general(a, b, (((1,), (0,)), ((), ())), preferred_element_type=F32)


def dot_tn(a, b):
    return lax.dot_general(a, b, (((0,), (0,)), ((), ())), preferred_element_type=F32)


def pair(queries, keys, bias, want_query, want_key):
    scale = queries.query.shape[1] ** (-0.5)
    scores = dot_nt(keys.key, queries.query)
    dprob = dot_nt(keys.value, queries.grad)
    tiles = scores.shape[0] // TILE
    probs = []
    for tile in range(tiles):
        part = scores[tile * TILE : (tile + 1) * TILE]
        probs.append(jnp.exp2(part * (scale * LOG2E) - (queries.norm + bias[tile])))
    prob = jnp.concatenate(probs, axis=0)
    dscore = (prob * (dprob - queries.delta)).astype(BF16)
    out = []
    if want_query:
        out.append(dot_tn(dscore, keys.key))
    if want_key:
        out.append(dot_nn(dscore, queries.query))
        out.append(dot_nn(prob.astype(BF16), queries.grad))
    return out


def bias_rows(bias_ref, index, tiles):
    return [bias_ref[index * tiles + t : index * tiles + t + 1] for t in range(tiles)]


def add_to(ref, value, first):
    if first:
        ref[...] = value
    else:
        ref[...] += value


def own_kernel(plan, place_ref, mask_ref, frame_ref, all_ref, mate_ref, bias_ref, dq_ref, dk_ref, dv_ref):
    rows = dq_ref.shape[0]
    tiles = rows // TILE
    levels = mask_ref.shape[0]
    slab = place_ref[0]
    space = place_ref[1]
    n_space = plan.n_space
    n_y = plan.n_y
    y = slab // 4
    x = (slab // 2) % 2
    core = slab % 2

    def write(index, flags):
        for b in range(tiles):
            line = []
            for a in range(tiles):
                far = jnp.where(flags[a][b] > 0, 0.0, FAR)
                line.append(jnp.full((1, TILE), far, F32))
            bias_ref[index * tiles + b : index * tiles + b + 1] = jnp.concatenate(line, axis=1)

    def frame(d, flip_x, flip_core):
        at_y = (y + d) % n_y
        at_x = x if not flip_x else 1 - x
        at_core = core if not flip_core else 1 - core
        return frame_ref[at_y * 4 + at_x * 2 + at_core]

    for index, (query_at, key_at) in enumerate(plan.pairs):
        distance = jnp.abs(frame(0, *query_at) - frame(key_at[0], 0, key_at[1]))
        level = jnp.int32(0)
        for power in range(levels - 1):
            level = level + jnp.where(distance >= (1 << power), 1, 0)
        base = space * tiles
        flags = [[mask_ref[level, base + a, base + b] for b in range(tiles)] for a in range(tiles)]
        write(index, flags)
    index = len(plan.pairs)
    for parity in range(2):
        up = (space % 2) == parity
        other = jnp.where(up, space + 1, space - 1)
        there = jnp.logical_and(other >= 0, other < n_space)
        other = jnp.clip(other, 0, n_space - 1)
        for mine_first in (True, False):
            at_q = (space if mine_first else other) * tiles
            at_k = (other if mine_first else space) * tiles
            flags = [
                [jnp.where(there, mask_ref[0, at_q + a, at_k + b], 0) for b in range(tiles)]
                for a in range(tiles)
            ]
            write(index, flags)
            index += 1

    base = 2 * rows + STAT_ROWS
    queries = Queries(all_ref, rows)
    keys = Keys(all_ref, rows, base)
    mate_queries = Queries(mate_ref, rows)
    mate_keys = Keys(mate_ref, rows, base)
    bias = functools.partial(bias_rows, bias_ref, tiles=tiles)
    own = ((0, 0), (0, 0))
    dq, dk, dv = pair(queries, keys, bias(plan.at(*own)), True, True)
    (more,) = pair(queries, mate_keys, bias(plan.at((0, 0), (0, 1))), True, False)
    dq_ref[...] = dq + more
    more_k, more_v = pair(mate_queries, keys, bias(plan.at((0, 1), (0, 0))), False, True)
    dk_ref[...] = dk + more_k
    dv_ref[...] = dv + more_v


def cross_kernel(plan, d_list, bias_ref, all_ref, mate_ref, x_ref, xm_ref, *refs):
    n = len(d_list)
    y_refs, ym_refs = refs[:n], refs[n : 2 * n]
    dqx_ref, dq_ref, dk_ref, dv_ref = refs[2 * n : 2 * n + 4]
    back_refs = refs[2 * n + 4 :]
    rows = dq_ref.shape[0]
    tiles = rows // TILE
    scale = dq_ref.shape[1] ** (-0.5)
    base = 2 * rows + STAT_ROWS
    bias = functools.partial(bias_rows, bias_ref, tiles=tiles)
    queries = Queries(all_ref, rows)
    keys = Keys(all_ref, rows, base)
    mate_queries = Queries(mate_ref, rows)
    mate_keys = Keys(mate_ref, rows, base)
    x_queries = Queries(x_ref, rows)
    xm_queries = Queries(xm_ref, rows)
    dqx, dk, dv = pair(x_queries, keys, bias(plan.at((1, 0), (0, 0))), True, True)
    dk_ref[...] = dk
    dv_ref[...] = dv
    (more,) = pair(x_queries, mate_keys, bias(plan.at((1, 0), (0, 1))), True, False)
    dqx = dqx + more
    dq = None
    for d, y_ref, ym_ref, back_ref in zip(d_list, y_refs, ym_refs, back_refs):
        y_keys = Keys(y_ref, rows)
        ym_keys = Keys(ym_ref, rows)
        q_part, k_part, v_part = pair(queries, y_keys, bias(plan.at((0, 0), (d, 0))), True, True)
        dq = q_part if dq is None else dq + q_part
        for source, at in ((mate_queries, (0, 1)), (x_queries, (1, 0)), (xm_queries, (1, 1))):
            mine = at[1] == 0
            got = pair(source, y_keys, bias(plan.at(at, (d, 0))), mine, True)
            if mine:
                dqx = dqx + got[0]
            k_part = k_part + got[-2]
            v_part = v_part + got[-1]
        back_ref[0:rows] = (k_part * scale).astype(BF16)
        back_ref[rows : 2 * rows] = v_part.astype(BF16)
        (more,) = pair(x_queries, ym_keys, bias(plan.at((1, 0), (d, 1))), True, False)
        dqx = dqx + more
    dq_ref[...] = dq
    dqx_ref[...] = (dqx * scale).astype(BF16)


def rest_kernel(plan, d_list, bias_ref, all_ref, xm_ref, za_ref, zb_ref, *refs):
    n = len(d_list)
    ym_refs = refs[:n]
    dq0_ref, dk0_ref, dv0_ref, dq1_ref, dk1_ref, dv1_ref = refs[n : n + 6]
    dq_ref, dk_ref, dv_ref = refs[n + 6 :]
    rows = dq_ref.shape[0]
    tiles = rows // TILE
    base = 2 * rows + STAT_ROWS
    bias = functools.partial(bias_rows, bias_ref, tiles=tiles)
    queries = Queries(all_ref, rows)
    keys = Keys(all_ref, rows, base)
    xm_queries = Queries(xm_ref, rows)
    dq = dq0_ref[...] + dq1_ref[...]
    dk, dv = pair(xm_queries, keys, bias(plan.at((1, 1), (0, 0))), False, True)
    dk = dk + dk0_ref[...] + dk1_ref[...]
    dv = dv + dv0_ref[...] + dv1_ref[...]
    for d, ym_ref in zip(d_list, ym_refs):
        (more,) = pair(queries, Keys(ym_ref, rows), bias(plan.at((0, 0), (d, 1))), True, False)
        dq = dq + more
    index = len(plan.pairs)
    for z_ref in (za_ref, zb_ref):
        (more,) = pair(queries, Keys(z_ref, rows, base), bias(index), True, False)
        dq = dq + more
        more_k, more_v = pair(Queries(z_ref, rows), keys, bias(index + 1), False, True)
        dk = dk + more_k
        dv = dv + more_v
        index += 2
    dq_ref[...] = dq
    dk_ref[...] = dk
    dv_ref[...] = dv


def last_kernel(n, dq_ref, dk_ref, dv_ref, x_ref, *refs):
    back_refs = refs[:n]
    out_q, out_k, out_v = refs[n:]
    rows = dq_ref.shape[0]
    scale = dq_ref.shape[1] ** (-0.5)
    dk = dk_ref[...] * scale
    dv = dv_ref[...]
    for back_ref in back_refs:
        dk = dk + back_ref[0:rows].astype(F32)
        dv = dv + back_ref[rows : 2 * rows].astype(F32)
    out_q[...] = (dq_ref[...] * scale + x_ref[...].astype(F32)).astype(BF16)
    out_k[...] = dk.astype(BF16)
    out_v[...] = dv.astype(BF16)


class Plan:
    def __init__(self, n_slab, n_space):
        assert n_slab % 4 == 0, n_slab
        self.n_space = n_space
        self.n_y = n_slab // 4
        self.pairs = []
        for query_at in ((0, 0), (0, 1), (1, 0), (1, 1)):
            for d in range(self.n_y):
                for core in range(2):
                    if query_at[1] + core < 2:
                        self.pairs.append((query_at, (d, core)))

    def at(self, query_at, key_at):
        return self.pairs.index((query_at, key_at))


def body(query_rows, key_rows, value_rows, out_saved, grad_out, log_norm, band_mask, frame_of_slab):
    rows, width = query_rows.shape
    assert log_norm.shape[0] == 1 and rows % TILE == 0
    n_slab = lax.axis_size("slab")
    n_space = lax.axis_size("space")
    plan = Plan(n_slab, n_space)
    n_y = plan.n_y
    tiles = rows // TILE
    place = jnp.stack([lax.axis_index("slab"), lax.axis_index("space")]).astype(jnp.int32)

    def along_slab(block, source_of):
        return lax.ppermute(block, "slab", [(source_of(i), i) for i in range(n_slab)])

    def other_core(block):
        return along_slab(block, lambda i: i ^ 1)

    def other_x(block):
        return along_slab(block, lambda i: i ^ 2)

    def from_y(block, d):
        return along_slab(block, lambda i: (i // 4 + d) % n_y * 4 + i % 4)

    def matched(block, first):
        pairs = [(i, i + 1) for i in range(first, n_space - 1, 2)]
        return lax.ppermute(block, "space", pairs + [(b, a) for a, b in pairs])

    def shape(dims, kind=F32):
        return jax.ShapeDtypeStruct(dims, kind)

    def call(kernel, out_shape, specs, *operands, flops=0):
        return pl.pallas_call(
            kernel,
            out_shape=out_shape,
            in_specs=specs,
            out_specs=jax.tree.map(lambda _: VMEM, out_shape),
            cost_estimate=pl.CostEstimate(
                flops=flops, bytes_accessed=1 << 20, transcendentals=0
            ),
        )(*operands)

    query_part = 2 * rows + STAT_ROWS
    packed_q, packed_k, packed = call(
        pack_kernel,
        (shape((query_part, width), BF16), shape((2 * rows, width), BF16), shape((query_part + 2 * rows, width), BF16)),
        [VMEM] * 6,
        query_rows, key_rows, value_rows, out_saved, grad_out, log_norm,
    )
    offsets = list(range(1, n_y))
    mate = other_core(packed)
    y_keys = [from_y(packed_k, d) for d in offsets]
    x_queries = other_x(packed_q)
    z_a = matched(packed, 0)
    z_b = matched(packed, 1)
    full = shape((rows, width))
    bias, dq0, dk0, dv0 = call(
        functools.partial(own_kernel, plan),
        (shape(((len(plan.pairs) + 4) * tiles, rows)), full, full, full),
        [SMEM, SMEM, SMEM, VMEM, VMEM],
        place, band_mask, frame_of_slab, packed, mate,
    )
    ym_keys = [other_core(block) for block in y_keys]
    xm_queries = other_core(x_queries)
    half = shape((rows, width), BF16)
    two = shape((2 * rows, width), BF16)
    got = call(
        functools.partial(cross_kernel, plan, offsets),
        (half, full, full, full) + (two,) * len(offsets),
        [VMEM] * (5 + 2 * len(offsets)),
        bias, packed, mate, x_queries, xm_queries, *y_keys, *ym_keys,
    )
    dqx, dq1, dk1, dv1 = got[:4]
    backs = [along_slab(back, lambda i, d=d: (i // 4 - d) % n_y * 4 + i % 4) for d, back in zip(offsets, got[4:])]
    x_back = other_x(dqx)
    dq, dk, dv = call(
        functools.partial(rest_kernel, plan, offsets),
        (full, full, full),
        [VMEM] * (11 + len(offsets)),
        bias, packed, xm_queries, z_a, z_b, *ym_keys, dq0, dk0, dv0, dq1, dk1, dv1,
    )
    return call(
        functools.partial(last_kernel, len(offsets)),
        (half, half, half),
        [VMEM] * (4 + len(offsets)),
        dq, dk, dv, x_back, *backs,
    )


def solution(mesh):
    split = P(("slab", "space"), None)
    return jax.shard_map(
        body,
        mesh=mesh,
        in_specs=(split, split, split, split, split, P(None, ("slab", "space")), P(), P()),
        out_specs=(split, split, split),
        check_vma=False,
    )
```
